32 devices in a mesh: gx: 8 (over y, x, core), gy: 4 (over z).
Axes of the slice: x: 2, y: 2, z: 4, core: 2. Of those that a mesh axis runs over, the one named last changes fastest.
Arguments:
- wind_u: float32 [96, 128, 1024], P('gy', 'gx'), may hold values from -6 to 6
- wind_v: float32 [96, 128, 1024], P('gy', 'gx'), may hold values from -6 to 6
- pressure: float32 [96, 128, 1024], P(None, 'gx', 'gy'), may hold values from -6 to 6
- vertical_w: float32 [96, 128, 1024], P(None, 'gx', 'gy'), may hold values from -6 to 6
- theta: float32 [96, 128, 1024], P(None, 'gx', 'gy'), may hold values from -6 to 6
- terrain: int32 [128, 1024], P('gx', 'gy'), may hold values from 0 to 3
- inverses: float32 [4, 192, 192], replicated, may hold values from -1 to 2, as said below
Outputs:
- wind_u_out: float32 [96, 128, 1024], P('gy', 'gx')
- wind_v_out: float32 [96, 128, 1024], P('gy', 'gx')
- pressure_out: float32 [96, 128, 1024], P(None, 'gx', 'gy')
- vertical_w_out: float32 [96, 128, 1024], P(None, 'gx', 'gy')
- theta_out: float32 [96, 128, 1024], P(None, 'gx', 'gy')
The draws below stay inside these ranges and needn't reach their ends.
Inputs may be any that keep to these rules, and one draw needn't show every extreme that they name: inverses has a diagonal between 0.6 and 1.6 and off-diagonal entries of order 1 / sqrt(192).
All inputs are finite; a program needn't handle non-finite values.
Results may differ from the reference program's by a relative error of at most 0.00013.
Values sent between devices are 32-bit elements; how exact they have to be, the bound alone decides.
A program may use at most 192 MiB of HBM per device.

```python
import jax
import jax.numpy as jnp
from jax import lax

NZ = 96
CLASSES = 4
SUBSTEPS = 4
NX = 128
NY = 1024


def draw_inverses(key, part):
    order_len = 2 * NZ
    first_key, second_key = jax.random.split(jax.random.fold_in(key, 17))
    diagonal = jax.random.uniform(first_key, (CLASSES, order_len), jnp.float32, 0.8, 1.2)
    spread = jax.random.uniform(second_key, (CLASSES, order_len, order_len), jnp.float32, -1.0, 1.0) * (0.9 / order_len ** 0.5)
    identity_mat = jnp.eye(order_len, dtype=jnp.float32)
    return spread * (1.0 - identity_mat) + diagonal[:, :, None] * identity_mat


def set_ends(result, stream_key, smallest, largest):
    longest = result.shape.index(max(result.shape))
    spots = []
    for shift in (0, 1):
        where = [jax.random.randint(jax.random.fold_in(stream_key, axis), (), 0, length) for axis, length in enumerate(result.shape)]
        where[longest] = (where[longest] + shift) % result.shape[longest]
        spots.append(tuple(where))
    return result.at[spots[0]].set(smallest).at[spots[1]].set(largest)


def shard_levels(key, dims, cuts, smallest, largest):
    loudness = 1.0
    for axis_at, blocks in cuts:
        heights = jax.random.uniform(jax.random.fold_in(jax.random.fold_in(key, 6), axis_at), (blocks,), jnp.float32, smallest / len(cuts), largest / len(cuts))
        loudness = loudness * jnp.repeat(jnp.exp(heights), dims[axis_at] // blocks).reshape((-1,) + (1,) * (len(dims) - 1 - axis_at))
    return loudness


def scatter_about(stream_key, dims, width, reach, pieces=(), kind=jnp.bfloat16):
    result = jax.random.normal(stream_key, dims, jnp.float32) * width
    if len(pieces) > 0:
        result = shard_levels(stream_key, dims, pieces, -0.22, 0.18) * result
    return jnp.clip(result, min=-reach, max=reach).astype(kind)


def setup_inputs(seed: int = 0) -> dict:
    splits = jax.random.split(jax.random.key(seed), 8)
    return {
        "wind_u": scatter_about(splits[0], (NZ, NX, NY), 1.0, 6.0, ((0, 4), (1, 8)), jnp.float32),
        "wind_v": scatter_about(splits[1], (NZ, NX, NY), 1.0, 6.0, ((0, 4), (1, 8)), jnp.float32),
        "pressure": scatter_about(splits[2], (NZ, NX, NY), 1.0, 6.0, ((1, 8), (2, 4)), jnp.float32),
        "vertical_w": scatter_about(splits[3], (NZ, NX, NY), 1.0, 6.0, ((1, 8), (2, 4)), jnp.float32),
        "theta": scatter_about(splits[4], (NZ, NX, NY), 1.0, 6.0, ((1, 8), (2, 4)), jnp.float32),
        "terrain": set_ends(jax.random.randint(splits[5], (NX, NY), 0, CLASSES), jax.random.fold_in(splits[5], 1), 0, CLASSES - 1).astype(jnp.int32),
        "inverses": draw_inverses(jax.random.fold_in(splits[7], 71), 0),
    }


def reference(wind_u, wind_v, pressure, vertical_w, theta, terrain, inverses):
    level_ids = lax.broadcasted_iota(jnp.int32, pressure.shape, 0)
    above = (level_ids >= terrain[None]).astype(jnp.float32)
    flat_terrain = terrain.reshape(-1)
    for step in range(SUBSTEPS):
        next_x = jnp.pad(pressure, ((0, 0), (0, 1), (0, 0)))[:, 1:]
        next_y = jnp.pad(pressure, ((0, 0), (0, 0), (0, 1)))[:, :, 1:]
        wind_u = wind_u - 0.5 * (next_x - pressure)
        wind_v = wind_v - 0.5 * (next_y - pressure)
        left_u = jnp.pad(wind_u, ((0, 0), (1, 0), (0, 0)))[:, :-1]
        left_v = jnp.pad(wind_v, ((0, 0), (0, 0), (1, 0)))[:, :, :-1]
        diverge = (wind_u - left_u) + (wind_v - left_v)
        below_p = jnp.pad(pressure, ((1, 0), (0, 0), (0, 0)))[:-1]
        rhs_w = vertical_w - 0.5 * (pressure - below_p)
        rhs_t = theta - 0.5 * diverge
        stacked = jnp.stack([rhs_w, rhs_t], axis=1).reshape(2 * NZ, NX * NY)
        solved = jnp.zeros_like(stacked)
        for klass in range(CLASSES):
            product = jnp.dot(inverses[klass], stacked, precision=lax.Precision.HIGHEST)
            solved = solved + jnp.where(flat_terrain[None] == klass, product, 0.0)
        solved = solved.reshape(NZ, 2, NX, NY)
        vertical_w = solved[:, 0] * above
        new_theta = solved[:, 1]
        pressure = pressure - 0.3 * diverge + 0.5 * (new_theta - theta)
        theta = new_theta
    return wind_u, wind_v, pressure, vertical_w, theta
```

```python
import functools

import jax
import jax.numpy as jnp
from jax import lax
from jax.experimental import pallas as pl
from jax.experimental.pallas import tpu as pltpu
from jax.sharding import PartitionSpec as P

SUBSTEPS = 4
MESH = pl.DeviceIdType.MESH
F32 = jnp.float32
BF16 = jnp.bfloat16


def kernel(dims, u_ref, v_ref, p_ref, w_ref, t_ref, terr_ref, inv_ref,
           uo_ref, vo_ref, po_ref, wo_ref, to_ref,
           u_buf, v_buf, p_buf, w_buf, t_buf, in_sem, out_sem,
           press, vert, theta, div, dsend, drecv, usend, uhalo,
           ysend, yhalo, ssend, srecv, shsend, shrecv, mats,
           d_s, d_r, u_s, u_r, y_s, y_r, x_s, x_r, s_s, s_r):
    ngx, ngy, nz, nx, ny, slab, classes = dims
    order = 2 * nz
    half = nx // 2
    turn = nx // 4
    wide = ngy * ny
    gx = lax.axis_index("gx")
    me = lax.axis_index("gy")
    has_left, has_right = gx > 0, gx < ngx - 1
    has_down, has_up = me > 0, me < ngy - 1

    def peer(r):
        return lax.rem(me + r, ngy)

    def at(dx, dy):
        return (gx + dx, me + dy)

    loads, stores = [], []
    for slot, (ref, buf, out) in enumerate((
            (u_ref, u_buf, uo_ref), (v_ref, v_buf, vo_ref), (p_ref, p_buf, po_ref),
            (w_ref, w_buf, wo_ref), (t_ref, t_buf, to_ref))):
        tiles = buf.shape[0]
        loads.append([pltpu.make_async_copy(
            ref.at[:, pl.ds(c * 128, 128)], buf.at[c], in_sem.at[slot, c]) for c in range(tiles)])
        stores.append([pltpu.make_async_copy(
            buf.at[c], out.at[:, pl.ds(c * 128, 128)], out_sem.at[slot, c]) for c in range(tiles)])

    def start(copies):
        for each in copies:
            each.start()

    def wait(copies):
        for each in copies:
            each.wait()

    def take(buf, i, count):
        parts = [buf[c, pl.ds(i, count, stride=nx), :] for c in range(buf.shape[0])]
        return jnp.concatenate(parts, axis=1)

    def put(buf, i, value):
        for c in range(buf.shape[0]):
            buf[c, pl.ds(i, value.shape[0], stride=nx), :] = value[:, c * 128:(c + 1) * 128]

    for each in loads:
        start(each)

    barrier = pltpu.get_barrier_semaphore()

    @pl.when(has_left)
    def _():
        pl.semaphore_signal(barrier, inc=1, device_id=at(-1, 0), device_id_type=MESH)

    @pl.when(has_right)
    def _():
        pl.semaphore_signal(barrier, inc=1, device_id=at(1, 0), device_id_type=MESH)

    for r in range(1, ngy):
        pl.semaphore_signal(barrier, inc=1, device_id=(gx, peer(r)), device_id_type=MESH)
    pl.semaphore_wait(barrier, ngy - 1 + has_left.astype(jnp.int32) + has_right.astype(jnp.int32))

    def copy(src, dst, send, recv, device):
        return pltpu.make_async_remote_copy(
            src_ref=src, dst_ref=dst, send_sem=send, recv_sem=recv,
            device_id=device, device_id_type=MESH)

    def x_copy(n, way):
        if way == 0:
            return copy(press.at[n, 1], press.at[n, nx + 1], x_s.at[n, 0], x_r.at[n, 0], at(-1, 0))
        return copy(press.at[n, nx], press.at[n, 0], x_s.at[n, 1], x_r.at[n, 1], at(1, 0))

    def y_copy(n, g, way):
        return copy(ysend.at[n, g, way], yhalo.at[n, g, way], y_s.at[n, g, way], y_r.at[n, g, way],
                    at(0, -1) if way == 0 else at(0, 1))

    def d_copy(g, r):
        return copy(dsend.at[g, peer(r)], drecv.at[g, me], d_s.at[g, r], d_r.at[g, r], (gx, peer(r)))

    def s_copy(g, r):
        return copy(ssend.at[g, peer(r)], srecv.at[g, me], s_s.at[g, r], s_r.at[g, r], (gx, peer(r)))

    def sh_copy(r):
        return copy(shsend.at[peer(r)], shrecv.at[me], s_s.at[2, r], s_r.at[2, r], (gx, peer(r)))

    def u_copy():
        return copy(usend, uhalo, u_s.at[0], u_r.at[0], at(1, 0))

    def x_start(n):
        pl.when(has_left)(lambda: x_copy(n, 0).start())
        pl.when(has_right)(lambda: x_copy(n, 1).start())

    def x_wait(n):
        @pl.when(has_right)
        def _():
            x_copy(n, 0).wait_recv()

        @pl.when(jnp.logical_not(has_right))
        def _():
            press[n, nx + 1] = jnp.zeros((nz, ny), F32)

        @pl.when(has_left)
        def _():
            x_copy(n, 1).wait_recv()

        @pl.when(jnp.logical_not(has_left))
        def _():
            press[n, 0] = press[n, 1]

    def y_start(n, g):
        pl.when(has_down)(lambda: y_copy(n, g, 0).start())
        pl.when(has_up)(lambda: y_copy(n, g, 1).start())

    def y_wait(n, g):
        pl.when(has_up)(lambda: y_copy(n, g, 0).wait_recv())
        pl.when(has_down)(lambda: y_copy(n, g, 1).wait_recv())

    lane = lax.broadcasted_iota(jnp.int32, (nz, 128), 1)
    lanes = lax.broadcasted_iota(jnp.int32, (nz, ny), 1)
    level = lax.broadcasted_iota(jnp.int32, (nz, ny), 0)
    wide_lane = lax.broadcasted_iota(jnp.int32, (slab, wide), 1)

    def plane(k):
        return lax.rem(k + turn, nx)

    def keep_edges(n, g, i, value):
        for way, column in ((0, 0), (1, ny - 1)):
            edge = jnp.broadcast_to(value[:, column:column + 1], (nz, 128))
            ysend[n, g, way] = jnp.where(lane == i, edge, ysend[n, g, way])

    def clear_edges(n, g):
        for way in (0, 1):
            ysend[n, g, way] = jnp.zeros((nz, 128), F32)

    wait(loads[0])
    usend[...] = take(u_buf, nx - 1, slab)
    pl.when(has_right)(lambda: u_copy().start())

    @pl.when(jnp.logical_not(has_left))
    def _():
        uhalo[...] = jnp.zeros((slab, wide), F32)

    for n in range(SUBSTEPS):
        for g in range(2):
            @pl.when(jnp.logical_not(has_up))
            def _():
                yhalo[n, g, 0] = jnp.zeros((nz, 128), F32)

            @pl.when(jnp.logical_not(has_down))
            def _():
                yhalo[n, g, 1] = jnp.zeros((nz, 128), F32)

    wait(loads[1])
    for g in range(2):
        if g == 1:
            pl.when(has_left)(lambda: u_copy().wait_recv())

        def first_div(kk, carry):
            i = plane(g * half + kk)
            here = take(u_buf, i, slab)
            left = take(u_buf, jnp.maximum(i - 1, 0), slab)
            if g == 1:
                left = jnp.where(i == 0, uhalo[...], left)
            v = take(v_buf, i, slab)
            left_v = jnp.where(wide_lane == 0, 0.0, pltpu.roll(v, 1, 1))
            d = here - left + (v - left_v)
            for q in range(ngy):
                dsend[g, q, kk] = d[:, q * ny:(q + 1) * ny]
            return carry

        lax.fori_loop(0, half, first_div, 0)
        for r in range(1, ngy):
            d_copy(g, r).start()
        drecv[g, me] = dsend[g, me]

    for each in loads[2:]:
        wait(each)
    for g in range(2):
        clear_edges(0, g)

        def relay(kk, carry):
            i = plane(g * half + kk)
            p = take(p_buf, i, nz)
            press[0, i + 1] = p
            vert[i] = take(w_buf, i, nz)
            theta[i] = take(t_buf, i, nz)
            keep_edges(0, g, i, p)
            return carry

        lax.fori_loop(0, half, relay, 0)
        y_start(0, g)
    x_start(0)

    rows = lax.broadcasted_iota(jnp.int32, (order, order), 0)
    cols = lax.broadcasted_iota(jnp.int32, (order, order), 1)

    def source(r):
        return jnp.where(r < nz, 2 * r, 2 * (r - nz) + 1)

    pick = (cols == source(rows)).astype(F32).astype(BF16)
    wide_rows = lax.broadcasted_iota(jnp.int32, (order, classes * order), 0)
    wide_cols = lax.broadcasted_iota(jnp.int32, (order, classes * order), 1)
    for part in range(2):
        total = jnp.zeros((order, classes * order), F32)
        for c in range(classes):
            a = inv_ref[c]
            a_hi = a.astype(BF16)
            a_part = a_hi if part == 0 else (a - a_hi.astype(F32)).astype(BF16)
            by_row = jnp.dot(pick, a_part, preferred_element_type=F32).astype(BF16)
            r = wide_cols - c * order
            place = (r >= 0) & (r < order) & (wide_rows == source(r))
            total = total + jnp.dot(by_row, place.astype(F32).astype(BF16), preferred_element_type=F32)
        mats[part * order:(part + 1) * order, :] = total.astype(BF16)

    for n in range(SUBSTEPS):
        last = n == SUBSTEPS - 1
        for g in range(2):
            if not last:
                clear_edges(n + 1, g)
            y_wait(n, g)
            if g == 1:
                x_wait(n)
            if n == 0:
                for r in range(1, ngy):
                    d_copy(g, r).wait_recv()
            if last and g == 1:
                edge = press[0, nx + 1]
                for m in range(1, SUBSTEPS):
                    edge = edge + press[m, nx + 1]
                for q in range(ngy):
                    shsend[q] = edge[q * slab:(q + 1) * slab]
                for r in range(1, ngy):
                    sh_copy(r).start()
                shrecv[me] = shsend[me]

            def substep(kk, carry):
                i = plane(g * half + kk)
                p = press[n, i + 1]
                up = pltpu.roll(p, ny - 1, 1)
                edge = pltpu.roll(yhalo[n, g, 0], 127 - i, 1)
                up = jnp.where(lanes == ny - 1, jnp.concatenate([edge] * (ny // 128), axis=1), up)
                down = pltpu.roll(p, 1, 1)
                edge = pltpu.roll(yhalo[n, g, 1], lax.rem(128 - i, 128), 1)
                edge = jnp.concatenate([edge] * (ny // 128), axis=1)
                edge = jnp.where(has_down, edge, p)
                down = jnp.where(lanes == 0, edge, down)
                if n == 0:
                    d = jnp.concatenate([drecv[g, q, kk] for q in range(ngy)], axis=0)
                else:
                    d = div[i]
                d = d - 0.5 * ((press[n, i + 2] - p) - (p - press[n, i]) + ((up - p) - (p - down)))
                if not last:
                    div[i] = d
                below = jnp.where(level == 0, 0.0, pltpu.roll(p, 1, 0))
                t = theta[i]
                rw = vert[i] - 0.5 * (p - below)
                rt = t - 0.5 * d
                s = jnp.concatenate([rw, rt], axis=0)
                hi = s.astype(BF16)
                lo = (s - hi.astype(F32)).astype(BF16)
                ground = terr_ref[pl.ds(i, 1), :]
                masks = [(ground == c).astype(F32).astype(BF16) for c in range(classes)]
                his = jnp.concatenate([hi * m for m in masks], axis=0)
                los = jnp.concatenate([lo * m for m in masks], axis=0)
                first = jnp.dot(mats[...], his, preferred_element_type=F32)
                second = jnp.dot(mats[:order, :], los, preferred_element_type=F32)
                solved = first[:order] + (first[order:] + second)
                st = solved[nz:]
                w = jnp.where(level >= ground, solved[:nz], 0.0)
                new_p = p - 0.3 * d + 0.5 * (st - t)
                if last:
                    put(p_buf, i, new_p)
                    put(w_buf, i, w)
                    put(t_buf, i, st)
                else:
                    press[n + 1, i + 1] = new_p
                    vert[i] = w
                    theta[i] = st
                    keep_edges(n + 1, g, i, new_p)
                if n == SUBSTEPS - 2:
                    total = new_p + p
                    for m in range(SUBSTEPS - 2):
                        total = total + press[m, i + 1]
                    for q in range(ngy):
                        ssend[g, q, kk] = total[q * slab:(q + 1) * slab]
                return carry

            lax.fori_loop(0, half, substep, 0)
            if not last:
                y_start(n + 1, g)
                if g == 1:
                    x_start(n + 1)
            if n == SUBSTEPS - 2:
                for r in range(1, ngy):
                    s_copy(g, r).start()
                srecv[g, me] = ssend[g, me]

    for each in stores[2:]:
        start(each)
    for g in range(2):
        for r in range(1, ngy):
            s_copy(g, r).wait_recv()
    for r in range(1, ngy):
        sh_copy(r).wait_recv()

    def summed(i):
        if i == nx:
            return jnp.concatenate([shrecv[q] for q in range(ngy)], axis=1)
        g, kk = divmod((i - turn) % nx, half)
        return jnp.concatenate([srecv[g, q, kk] for q in range(ngy)], axis=1)

    for i in range(nx):
        s = summed(i)
        ahead = jnp.where(wide_lane == wide - 1, 0.0, pltpu.roll(s, wide - 1, 1))
        put(u_buf, i, take(u_buf, i, slab) - 0.5 * (summed(i + 1) - s))
        put(v_buf, i, take(v_buf, i, slab) - 0.5 * (ahead - s))
    start(stores[0])
    start(stores[1])

    pl.when(has_right)(lambda: u_copy().wait_send())
    for n in range(SUBSTEPS):
        pl.when(has_left)(lambda: x_copy(n, 0).wait_send())
        pl.when(has_right)(lambda: x_copy(n, 1).wait_send())
        for g in range(2):
            pl.when(has_down)(lambda: y_copy(n, g, 0).wait_send())
            pl.when(has_up)(lambda: y_copy(n, g, 1).wait_send())
    for r in range(1, ngy):
        for g in range(2):
            d_copy(g, r).wait_send()
            s_copy(g, r).wait_send()
        sh_copy(r).wait_send()
    for each in stores:
        wait(each)


def per_device(wind_u, wind_v, pressure, vertical_w, theta, terrain, inverses):
    ngx, ngy = lax.axis_size("gx"), lax.axis_size("gy")
    nz, nx, ny = pressure.shape
    slab, _, wide = wind_u.shape
    classes = inverses.shape[0]
    order = 2 * nz
    half = nx // 2
    vmem = pl.BlockSpec(memory_space=pltpu.VMEM)
    hbm = pl.BlockSpec(memory_space=pl.ANY)
    slabs = jax.ShapeDtypeStruct((slab * nx, wide), F32)
    columns = jax.ShapeDtypeStruct((nz * nx, ny), F32)
    dma = pltpu.SemaphoreType.DMA
    outs = pl.pallas_call(
        functools.partial(kernel, (ngx, ngy, nz, nx, ny, slab, classes)),
        out_shape=(slabs, slabs, columns, columns, columns),
        in_specs=[hbm] * 5 + [vmem] * 2,
        out_specs=(hbm,) * 5,
        scratch_shapes=[
            pltpu.VMEM((wide // 128, slab * nx, 128), F32),
            pltpu.VMEM((wide // 128, slab * nx, 128), F32),
            pltpu.VMEM((ny // 128, nz * nx, 128), F32),
            pltpu.VMEM((ny // 128, nz * nx, 128), F32),
            pltpu.VMEM((ny // 128, nz * nx, 128), F32),
            dma((5, wide // 128)), dma((5, wide // 128)),
            pltpu.VMEM((SUBSTEPS, nx + 2, nz, ny), F32),
            pltpu.VMEM((nx, nz, ny), F32),
            pltpu.VMEM((nx, nz, ny), F32),
            pltpu.VMEM((nx, nz, ny), F32),
            pltpu.VMEM((2, ngy, half, slab, ny), F32),
            pltpu.VMEM((2, ngy, half, slab, ny), F32),
            pltpu.VMEM((slab, wide), F32),
            pltpu.VMEM((slab, wide), F32),
            pltpu.VMEM((SUBSTEPS, 2, 2, nz, 128), F32),
            pltpu.VMEM((SUBSTEPS, 2, 2, nz, 128), F32),
            pltpu.VMEM((2, ngy, half, slab, ny), F32),
            pltpu.VMEM((2, ngy, half, slab, ny), F32),
            pltpu.VMEM((ngy, slab, ny), F32),
            pltpu.VMEM((ngy, slab, ny), F32),
            pltpu.VMEM((2 * order, classes * order), BF16),
            dma((2, ngy)), dma((2, ngy)),
            dma((1,)), dma((1,)),
            dma((SUBSTEPS, 2, 2)), dma((SUBSTEPS, 2, 2)),
            dma((SUBSTEPS, 2)), dma((SUBSTEPS, 2)),
            dma((3, ngy)), dma((3, ngy)),
        ],
        compiler_params=pltpu.CompilerParams(
            collective_id=0, has_side_effects=True, vmem_limit_bytes=60 * 1024 * 1024),
        name="acoustic",
    )(
        wind_u.reshape(slab * nx, wide), wind_v.reshape(slab * nx, wide),
        pressure.reshape(nz * nx, ny), vertical_w.reshape(nz * nx, ny),
        theta.reshape(nz * nx, ny), terrain, inverses,
    )
    return (outs[0].reshape(slab, nx, wide), outs[1].reshape(slab, nx, wide),
            *(o.reshape(nz, nx, ny) for o in outs[2:]))


def solution(mesh):
    return jax.shard_map(
        per_device,
        mesh=mesh,
        in_specs=(
            P("gy", "gx", None),
            P("gy", "gx", None),
            P(None, "gx", "gy"),
            P(None, "gx", "gy"),
            P(None, "gx", "gy"),
            P("gx", "gy"),
            P(),
        ),
        out_specs=(
            P("gy", "gx", None),
            P("gy", "gx", None),
            P(None, "gx", "gy"),
            P(None, "gx", "gy"),
            P(None, "gx", "gy"),
        ),
        check_vma=False,
    )
```

```python
import functools

import jax
import jax.numpy as jnp
from jax import lax
from jax.experimental import pallas as pl
from jax.experimental.pallas import tpu as pltpu
from jax.sharding import PartitionSpec as P

SUBSTEPS = 4
MESH = pl.DeviceIdType.MESH
F32 = jnp.float32
BF16 = jnp.bfloat16


def kernel(dims, u_ref, v_ref, p_ref, w_ref, t_ref, terr_ref, inv_ref,
           u_buf, v_buf, p_buf, w_buf, t_buf, in_sem,
           press, vert, theta, div, dsend, drecv, usend, uhalo,
           ysend, yhalo, ssend, srecv, shsend, shrecv, mats,
           d_s, d_r, u_s, u_r, y_s, y_r, x_s, x_r, s_s, s_r):
    ngx, ngy, nz, nx, ny, slab, classes = dims
    order = 2 * nz
    half = nx // 2
    quarter = nx // 4
    turn = quarter
    wide = ngy * ny
    gx = lax.axis_index("gx")
    me = lax.axis_index("gy")
    has_left, has_right = gx > 0, gx < ngx - 1
    has_down, has_up = me > 0, me < ngy - 1

    def peer(r):
        return lax.rem(me + r, ngy)

    def at(dx, dy):
        return (gx + dx, me + dy)

    loads = []
    for slot, (ref, buf) in enumerate((
            (u_ref, u_buf), (v_ref, v_buf), (p_ref, p_buf), (w_ref, w_buf), (t_ref, t_buf))):
        tiles = buf.shape[0]
        loads.append([pltpu.make_async_copy(
            ref.at[:, pl.ds(c * 128, 128)], buf.at[c], in_sem.at[slot, c]) for c in range(tiles)])

    def start(copies):
        for each in copies:
            each.start()

    def wait(copies):
        for each in copies:
            each.wait()

    def take(buf, i, count):
        parts = [buf[c, pl.ds(i, count, stride=nx), :] for c in range(buf.shape[0])]
        return jnp.concatenate(parts, axis=1)

    def put(buf, i, value):
        for c in range(buf.shape[0]):
            buf[c, pl.ds(i, value.shape[0], stride=nx), :] = value[:, c * 128:(c + 1) * 128]

    for each in loads:
        start(each)

    barrier = pltpu.get_barrier_semaphore()

    @pl.when(has_left)
    def _():
        pl.semaphore_signal(barrier, inc=1, device_id=at(-1, 0), device_id_type=MESH)

    @pl.when(has_right)
    def _():
        pl.semaphore_signal(barrier, inc=1, device_id=at(1, 0), device_id_type=MESH)

    for r in range(1, ngy):
        pl.semaphore_signal(barrier, inc=1, device_id=(gx, peer(r)), device_id_type=MESH)
    pl.semaphore_wait(barrier, ngy - 1 + has_left.astype(jnp.int32) + has_right.astype(jnp.int32))

    def copy(src, dst, send, recv, device):
        return pltpu.make_async_remote_copy(
            src_ref=src, dst_ref=dst, send_sem=send, recv_sem=recv,
            device_id=device, device_id_type=MESH)

    def x_copy(n, way):
        if way == 0:
            return copy(press.at[n, 1], press.at[n, nx + 1], x_s.at[n, 0], x_r.at[n, 0], at(-1, 0))
        return copy(press.at[n, nx], press.at[n, 0], x_s.at[n, 1], x_r.at[n, 1], at(1, 0))

    def y_copy(n, g, way):
        return copy(ysend.at[n, g, way], yhalo.at[n, g, way], y_s.at[n, g, way], y_r.at[n, g, way],
                    at(0, -1) if way == 0 else at(0, 1))

    def d_copy(g, r):
        return copy(dsend.at[g, peer(r)], drecv.at[g, me], d_s.at[g, r], d_r.at[g, r], (gx, peer(r)))

    def s_copy(g, r):
        return copy(ssend.at[g, peer(r)], srecv.at[g, me], s_s.at[g, r], s_r.at[g, r], (gx, peer(r)))

    def sh_copy(r):
        return copy(shsend.at[peer(r)], shrecv.at[me], s_s.at[4, r], s_r.at[4, r], (gx, peer(r)))

    def u_copy():
        return copy(usend, uhalo, u_s.at[0], u_r.at[0], at(1, 0))

    def x_start(n):
        pl.when(has_left)(lambda: x_copy(n, 0).start())
        pl.when(has_right)(lambda: x_copy(n, 1).start())

    def x_wait(n):
        @pl.when(has_right)
        def _():
            x_copy(n, 0).wait_recv()

        @pl.when(jnp.logical_not(has_right))
        def _():
            press[n, nx + 1] = jnp.zeros((nz, ny), F32)

        @pl.when(has_left)
        def _():
            x_copy(n, 1).wait_recv()

        @pl.when(jnp.logical_not(has_left))
        def _():
            press[n, 0] = press[n, 1]

    def y_start(n, g):
        pl.when(has_down)(lambda: y_copy(n, g, 0).start())
        pl.when(has_up)(lambda: y_copy(n, g, 1).start())

    def y_wait(n, g):
        pl.when(has_up)(lambda: y_copy(n, g, 0).wait_recv())
        pl.when(has_down)(lambda: y_copy(n, g, 1).wait_recv())

    lane = lax.broadcasted_iota(jnp.int32, (nz, 128), 1)
    lanes = lax.broadcasted_iota(jnp.int32, (nz, ny), 1)
    level = lax.broadcasted_iota(jnp.int32, (nz, ny), 0)
    wide_lane = lax.broadcasted_iota(jnp.int32, (slab, wide), 1)

    def plane(k):
        return lax.rem(k + turn, nx)

    def keep_edges(n, g, i, value):
        for way, column in ((0, 0), (1, ny - 1)):
            edge = jnp.broadcast_to(value[:, column:column + 1], (nz, 128))
            ysend[n, g, way] = jnp.where(lane == i, edge, ysend[n, g, way])

    def clear_edges(n, g):
        for way in (0, 1):
            ysend[n, g, way] = jnp.zeros((nz, 128), F32)

    wait(loads[0])
    usend[...] = take(u_buf, nx - 1, slab)
    pl.when(has_right)(lambda: u_copy().start())

    @pl.when(jnp.logical_not(has_left))
    def _():
        uhalo[...] = jnp.zeros((slab, wide), F32)

    for n in range(SUBSTEPS):
        for g in range(2):
            @pl.when(jnp.logical_not(has_up))
            def _():
                yhalo[n, g, 0] = jnp.zeros((nz, 128), F32)

            @pl.when(jnp.logical_not(has_down))
            def _():
                yhalo[n, g, 1] = jnp.zeros((nz, 128), F32)

    wait(loads[1])
    for g in range(4):
        if g == 3:
            pl.when(has_left)(lambda: u_copy().wait_recv())

        def first_div(kk, carry):
            i = plane(g * quarter + kk)
            here = take(u_buf, i, slab)
            left = take(u_buf, jnp.maximum(i - 1, 0), slab)
            if g == 3:
                left = jnp.where(i == 0, uhalo[...], left)
            v = take(v_buf, i, slab)
            left_v = jnp.where(wide_lane == 0, 0.0, pltpu.roll(v, 1, 1))
            d = here - left + (v - left_v)
            for q in range(ngy):
                dsend[g, q, kk] = d[:, q * ny:(q + 1) * ny]
            return carry

        lax.fori_loop(0, quarter, first_div, 0, unroll=2)
        for r in range(1, ngy):
            d_copy(g, r).start()
        drecv[g, me] = dsend[g, me]

    for each in loads[2:]:
        wait(each)
    for g in range(2):
        clear_edges(0, g)

        def relay(kk, carry):
            i = plane(g * half + kk)
            p = take(p_buf, i, nz)
            press[0, i + 1] = p
            vert[i] = take(w_buf, i, nz)
            theta[i] = take(t_buf, i, nz)
            keep_edges(0, g, i, p)
            return carry

        lax.fori_loop(0, half, relay, 0, unroll=2)
        y_start(0, g)
    x_start(0)

    rows = lax.broadcasted_iota(jnp.int32, (order, order), 0)
    cols = lax.broadcasted_iota(jnp.int32, (order, order), 1)

    def source(r):
        return jnp.where(r < nz, 2 * r, 2 * (r - nz) + 1)

    pick = (cols == source(rows)).astype(F32).astype(BF16)
    wide_rows = lax.broadcasted_iota(jnp.int32, (order, classes * order), 0)
    wide_cols = lax.broadcasted_iota(jnp.int32, (order, classes * order), 1)
    for part in range(2):
        total = jnp.zeros((order, classes * order), F32)
        for c in range(classes):
            a = inv_ref[c]
            a_hi = a.astype(BF16)
            a_part = a_hi if part == 0 else (a - a_hi.astype(F32)).astype(BF16)
            by_row = jnp.dot(pick, a_part, preferred_element_type=F32).astype(BF16)
            r = wide_cols - c * order
            place = (r >= 0) & (r < order) & (wide_rows == source(r))
            total = total + jnp.dot(by_row, place.astype(F32).astype(BF16), preferred_element_type=F32)
        mats[part * order:(part + 1) * order, :] = total.astype(BF16)

    for n in range(SUBSTEPS):
        last = n == SUBSTEPS - 1
        for g in range(2):
            if not last:
                clear_edges(n + 1, g)
            if g == (0 if last else 1):
                x_wait(n)
            if last and g == 0:
                edge = press[0, nx + 1]
                for m in range(1, SUBSTEPS):
                    edge = edge + press[m, nx + 1]
                for q in range(ngy):
                    shsend[q] = edge[q * slab:(q + 1) * slab]
                for r in range(1, ngy):
                    sh_copy(r).start()
                shrecv[me] = shsend[me]
            y_wait(n, g)

            def substep(h, kk, carry):
                i = plane(h * quarter + kk)
                p = press[n, i + 1]
                up = pltpu.roll(p, ny - 1, 1)
                edge = pltpu.roll(yhalo[n, g, 0], 127 - i, 1)
                up = jnp.where(lanes == ny - 1, jnp.concatenate([edge] * (ny // 128), axis=1), up)
                down = pltpu.roll(p, 1, 1)
                edge = pltpu.roll(yhalo[n, g, 1], lax.rem(128 - i, 128), 1)
                edge = jnp.concatenate([edge] * (ny // 128), axis=1)
                edge = jnp.where(has_down, edge, p)
                down = jnp.where(lanes == 0, edge, down)
                if n == 0:
                    d = jnp.concatenate([drecv[h, q, kk] for q in range(ngy)], axis=0)
                else:
                    d = div[i]
                d = d - 0.5 * ((press[n, i + 2] - p) - (p - press[n, i]) + ((up - p) - (p - down)))
                if not last:
                    div[i] = d
                below = jnp.where(level == 0, 0.0, pltpu.roll(p, 1, 0))
                t = theta[i]
                rw = vert[i] - 0.5 * (p - below)
                rt = t - 0.5 * d
                s = jnp.concatenate([rw, rt], axis=0)
                hi = s.astype(BF16)
                lo = (s - hi.astype(F32)).astype(BF16)
                ground = terr_ref[pl.ds(i, 1), :]
                masks = [(ground == c).astype(F32).astype(BF16) for c in range(classes)]
                his = jnp.concatenate([hi * m for m in masks], axis=0)
                los = jnp.concatenate([lo * m for m in masks], axis=0)
                first = jnp.dot(mats[...], his, preferred_element_type=F32)
                second = jnp.dot(mats[:order, :], los, preferred_element_type=F32)
                solved = first[:order] + (first[order:] + second)
                st = solved[nz:]
                w = jnp.where(level >= ground, solved[:nz], 0.0)
                new_p = p - 0.3 * d + 0.5 * (st - t)
                if last:
                    put(p_buf, i, new_p)
                    put(w_buf, i, w)
                    put(t_buf, i, st)
                else:
                    press[n + 1, i + 1] = new_p
                    vert[i] = w
                    theta[i] = st
                    keep_edges(n + 1, g, i, new_p)
                if n == SUBSTEPS - 2:
                    total = new_p + p
                    for m in range(SUBSTEPS - 2):
                        total = total + press[m, i + 1]
                    for q in range(ngy):
                        ssend[h, q, kk] = total[q * slab:(q + 1) * slab]
                return carry

            for h in (2 * g, 2 * g + 1):
                if n == 0:
                    for r in range(1, ngy):
                        d_copy(h, r).wait_recv()
                lax.fori_loop(0, quarter, functools.partial(substep, h), 0, unroll=2)
                if not last and h == 2 * g + 1:
                    y_start(n + 1, g)
                    if g == 1:
                        x_start(n + 1)
                if n == SUBSTEPS - 2:
                    for r in range(1, ngy):
                        s_copy(h, r).start()
                    srecv[h, me] = ssend[h, me]

    def summed(i):
        if i == nx:
            return jnp.concatenate([shrecv[q] for q in range(ngy)], axis=1)
        g, kk = divmod((i - turn) % nx, quarter)
        return jnp.concatenate([srecv[g, q, kk] for q in range(ngy)], axis=1)

    def finish(i):
        s = summed(i)
        ahead = jnp.where(wide_lane == wide - 1, 0.0, pltpu.roll(s, wide - 1, 1))
        put(u_buf, i, take(u_buf, i, slab) - 0.5 * (summed(i + 1) - s))
        put(v_buf, i, take(v_buf, i, slab) - 0.5 * (ahead - s))

    for g in range(4):
        for r in range(1, ngy):
            s_copy(g, r).wait_recv()
        for k in range(max(g * quarter - 1, 0), (g + 1) * quarter - 1):
            if k != nx - 1 - turn:
                finish((k + turn) % nx)
    finish(turn - 1)
    for r in range(1, ngy):
        sh_copy(r).wait_recv()
    finish(nx - 1)

    pl.when(has_right)(lambda: u_copy().wait_send())
    for n in range(SUBSTEPS):
        pl.when(has_left)(lambda: x_copy(n, 0).wait_send())
        pl.when(has_right)(lambda: x_copy(n, 1).wait_send())
        for g in range(2):
            pl.when(has_down)(lambda: y_copy(n, g, 0).wait_send())
            pl.when(has_up)(lambda: y_copy(n, g, 1).wait_send())
    for r in range(1, ngy):
        for g in range(4):
            d_copy(g, r).wait_send()
            s_copy(g, r).wait_send()
        sh_copy(r).wait_send()


def write_out(*refs):
    ins, outs, sem = refs[:5], refs[5:10], refs[10]
    copies = [
        pltpu.make_async_copy(buf.at[c], out.at[:, pl.ds(c * 128, 128)], sem.at[slot, c])
        for slot, (buf, out) in enumerate(zip(ins, outs)) for c in range(buf.shape[0])]
    for each in copies:
        each.start()
    for each in copies:
        each.wait()


def per_device(wind_u, wind_v, pressure, vertical_w, theta, terrain, inverses):
    ngx, ngy = lax.axis_size("gx"), lax.axis_size("gy")
    nz, nx, ny = pressure.shape
    slab, _, wide = wind_u.shape
    classes = inverses.shape[0]
    order = 2 * nz
    quarter = nx // 4
    vmem = pl.BlockSpec(memory_space=pltpu.VMEM)
    hbm = pl.BlockSpec(memory_space=pltpu.HBM)
    slabs = jax.ShapeDtypeStruct((wide // 128, slab * nx, 128), F32)
    columns = jax.ShapeDtypeStruct((ny // 128, nz * nx, 128), F32)
    dma = pltpu.SemaphoreType.DMA
    outs = pl.pallas_call(
        functools.partial(kernel, (ngx, ngy, nz, nx, ny, slab, classes)),
        out_shape=(slabs, slabs, columns, columns, columns),
        in_specs=[hbm] * 5 + [vmem] * 2,
        out_specs=(vmem,) * 5,
        scratch_shapes=[
            dma((5, wide // 128)),
            pltpu.VMEM((SUBSTEPS, nx + 2, nz, ny), F32),
            pltpu.VMEM((nx, nz, ny), F32),
            pltpu.VMEM((nx, nz, ny), F32),
            pltpu.VMEM((nx, nz, ny), F32),
            pltpu.VMEM((4, ngy, quarter, slab, ny), F32),
            pltpu.VMEM((4, ngy, quarter, slab, ny), F32),
            pltpu.VMEM((slab, wide), F32),
            pltpu.VMEM((slab, wide), F32),
            pltpu.VMEM((SUBSTEPS, 2, 2, nz, 128), F32),
            pltpu.VMEM((SUBSTEPS, 2, 2, nz, 128), F32),
            pltpu.VMEM((4, ngy, quarter, slab, ny), F32),
            pltpu.VMEM((4, ngy, quarter, slab, ny), F32),
            pltpu.VMEM((ngy, slab, ny), F32),
            pltpu.VMEM((ngy, slab, ny), F32),
            pltpu.VMEM((2 * order, classes * order), BF16),
            dma((4, ngy)), dma((4, ngy)),
            dma((1,)), dma((1,)),
            dma((SUBSTEPS, 2, 2)), dma((SUBSTEPS, 2, 2)),
            dma((SUBSTEPS, 2)), dma((SUBSTEPS, 2)),
            dma((5, ngy)), dma((5, ngy)),
        ],
        compiler_params=pltpu.CompilerParams(
            collective_id=0, has_side_effects=True, vmem_limit_bytes=52 * 1024 * 1024),
        name="acoustic",
    )(
        wind_u.reshape(slab * nx, wide), wind_v.reshape(slab * nx, wide),
        pressure.reshape(nz * nx, ny), vertical_w.reshape(nz * nx, ny),
        theta.reshape(nz * nx, ny), terrain, inverses,
    )
    outs = pl.pallas_call(
        write_out,
        out_shape=tuple(jax.ShapeDtypeStruct((o.shape[1], o.shape[0] * 128), F32) for o in outs),
        in_specs=[vmem] * 5,
        out_specs=(hbm,) * 5,
        scratch_shapes=[dma((5, wide // 128))],
        compiler_params=pltpu.CompilerParams(vmem_limit_bytes=16 * 1024 * 1024),
        name="write_out",
    )(*outs)
    return (outs[0].reshape(slab, nx, wide), outs[1].reshape(slab, nx, wide),
            *(o.reshape(nz, nx, ny) for o in outs[2:]))


def solution(mesh):
    return jax.shard_map(
        per_device,
        mesh=mesh,
        in_specs=(
            P("gy", "gx", None),
            P("gy", "gx", None),
            P(None, "gx", "gy"),
            P(None, "gx", "gy"),
            P(None, "gx", "gy"),
            P("gx", "gy"),
            P(),
        ),
        out_specs=(
            P("gy", "gx", None),
            P("gy", "gx", None),
            P(None, "gx", "gy"),
            P(None, "gx", "gy"),
            P(None, "gx", "gy"),
        ),
        check_vma=False,
    )
```

```python
import functools

import jax
import jax.numpy as jnp
from jax import lax
from jax.experimental import pallas as pl
from jax.experimental.pallas import tpu as pltpu
from jax.sharding import PartitionSpec as P

SUBSTEPS = 4
MESH = pl.DeviceIdType.MESH
F32 = jnp.float32
BF16 = jnp.bfloat16


def kernel(dims, u_ref, v_ref, p_ref, w_ref, t_ref, terr_hbm, inv_hbm,
           u_buf, v_buf, p_buf, w_buf, t_buf, terr_ref, inv_ref, in_sem, small_sem,
           press, vert, theta, div, dsend, drecv, usend, uhalo,
           ysend, yhalo, ssend, srecv, shsend, shrecv, mats,
           d_s, d_r, u_s, u_r, y_s, y_r, x_s, x_r, s_s, s_r):
    ngx, ngy, nz, nx, ny, slab, classes = dims
    order = 2 * nz
    half = nx // 2
    quarter = nx // 4
    turn = quarter
    wide = ngy * ny
    gx = lax.axis_index("gx")
    me = lax.axis_index("gy")
    has_left, has_right = gx > 0, gx < ngx - 1
    has_down, has_up = me > 0, me < ngy - 1

    def peer(r):
        return lax.rem(me + r, ngy)

    def at(dx, dy):
        return (gx + dx, me + dy)

    loads = []
    for slot, (ref, buf) in enumerate((
            (u_ref, u_buf), (v_ref, v_buf), (p_ref, p_buf), (w_ref, w_buf), (t_ref, t_buf))):
        tiles = buf.shape[0]
        loads.append([pltpu.make_async_copy(
            ref.at[:, pl.ds(c * 128, 128)], buf.at[c], in_sem.at[slot, c]) for c in range(tiles)])

    def start(copies):
        for each in copies:
            each.start()

    def wait(copies):
        for each in copies:
            each.wait()

    def take(buf, i, count):
        parts = [buf[c, pl.ds(i, count, stride=nx), :] for c in range(buf.shape[0])]
        return jnp.concatenate(parts, axis=1)

    def put(buf, i, value):
        for c in range(buf.shape[0]):
            buf[c, pl.ds(i, value.shape[0], stride=nx), :] = value[:, c * 128:(c + 1) * 128]

    loads.append([
        pltpu.make_async_copy(terr_hbm, terr_ref, small_sem.at[0]),
        pltpu.make_async_copy(inv_hbm, inv_ref, small_sem.at[1]),
    ])
    for each in loads:
        start(each)

    barrier = pltpu.get_barrier_semaphore()

    @pl.when(has_left)
    def _():
        pl.semaphore_signal(barrier, inc=1, device_id=at(-1, 0), device_id_type=MESH)

    @pl.when(has_right)
    def _():
        pl.semaphore_signal(barrier, inc=1, device_id=at(1, 0), device_id_type=MESH)

    for r in range(1, ngy):
        pl.semaphore_signal(barrier, inc=1, device_id=(gx, peer(r)), device_id_type=MESH)
    pl.semaphore_wait(barrier, ngy - 1 + has_left.astype(jnp.int32) + has_right.astype(jnp.int32))

    def copy(src, dst, send, recv, device):
        return pltpu.make_async_remote_copy(
            src_ref=src, dst_ref=dst, send_sem=send, recv_sem=recv,
            device_id=device, device_id_type=MESH)

    def x_copy(n, way):
        if way == 0:
            return copy(press.at[n, 1], press.at[n, nx + 1], x_s.at[n, 0], x_r.at[n, 0], at(-1, 0))
        return copy(press.at[n, nx], press.at[n, 0], x_s.at[n, 1], x_r.at[n, 1], at(1, 0))

    def y_copy(n, g, way):
        return copy(ysend.at[n, g, way], yhalo.at[n, g, way], y_s.at[n, g, way], y_r.at[n, g, way],
                    at(0, -1) if way == 0 else at(0, 1))

    def d_copy(g, r):
        return copy(dsend.at[g, peer(r)], drecv.at[g, me], d_s.at[g, r], d_r.at[g, r], (gx, peer(r)))

    def s_copy(g, r):
        return copy(ssend.at[g, peer(r)], srecv.at[g, me], s_s.at[g, r], s_r.at[g, r], (gx, peer(r)))

    def sh_copy(r):
        return copy(shsend.at[peer(r)], shrecv.at[me], s_s.at[4, r], s_r.at[4, r], (gx, peer(r)))

    def u_copy():
        return copy(usend, uhalo, u_s.at[0], u_r.at[0], at(1, 0))

    def x_start(n):
        pl.when(has_left)(lambda: x_copy(n, 0).start())
        pl.when(has_right)(lambda: x_copy(n, 1).start())

    def x_wait(n):
        @pl.when(has_right)
        def _():
            x_copy(n, 0).wait_recv()

        @pl.when(jnp.logical_not(has_right))
        def _():
            press[n, nx + 1] = jnp.zeros((nz, ny), F32)

        @pl.when(has_left)
        def _():
            x_copy(n, 1).wait_recv()

        @pl.when(jnp.logical_not(has_left))
        def _():
            press[n, 0] = press[n, 1]

    def y_start(n, g):
        pl.when(has_down)(lambda: y_copy(n, g, 0).start())
        pl.when(has_up)(lambda: y_copy(n, g, 1).start())

    def y_wait(n, g):
        pl.when(has_up)(lambda: y_copy(n, g, 0).wait_recv())
        pl.when(has_down)(lambda: y_copy(n, g, 1).wait_recv())

    lane = lax.broadcasted_iota(jnp.int32, (nz, 128), 1)
    lanes = lax.broadcasted_iota(jnp.int32, (nz, ny), 1)
    level = lax.broadcasted_iota(jnp.int32, (nz, ny), 0)
    wide_lane = lax.broadcasted_iota(jnp.int32, (slab, wide), 1)

    def plane(k):
        return lax.rem(k + turn, nx)

    def keep_edges(n, g, i, value):
        for way, column in ((0, 0), (1, ny - 1)):
            edge = jnp.broadcast_to(value[:, column:column + 1], (nz, 128))
            ysend[n, g, way] = jnp.where(lane == i, edge, ysend[n, g, way])

    def clear_edges(n, g):
        for way in (0, 1):
            ysend[n, g, way] = jnp.zeros((nz, 128), F32)

    wait(loads[0])
    usend[...] = take(u_buf, nx - 1, slab)
    pl.when(has_right)(lambda: u_copy().start())

    @pl.when(jnp.logical_not(has_left))
    def _():
        uhalo[...] = jnp.zeros((slab, wide), F32)

    for n in range(SUBSTEPS):
        for g in range(2):
            @pl.when(jnp.logical_not(has_up))
            def _():
                yhalo[n, g, 0] = jnp.zeros((nz, 128), F32)

            @pl.when(jnp.logical_not(has_down))
            def _():
                yhalo[n, g, 1] = jnp.zeros((nz, 128), F32)

    wait(loads[1])
    for g in range(4):
        if g == 3:
            pl.when(has_left)(lambda: u_copy().wait_recv())

        def first_div(kk, carry):
            i = plane(g * quarter + kk)
            here = take(u_buf, i, slab)
            left = take(u_buf, jnp.maximum(i - 1, 0), slab)
            if g == 3:
                left = jnp.where(i == 0, uhalo[...], left)
            v = take(v_buf, i, slab)
            left_v = jnp.where(wide_lane == 0, 0.0, pltpu.roll(v, 1, 1))
            d = here - left + (v - left_v)
            for q in range(ngy):
                dsend[g, q, kk] = d[:, q * ny:(q + 1) * ny]
            return carry

        lax.fori_loop(0, quarter, first_div, 0, unroll=2)
        for r in range(1, ngy):
            d_copy(g, r).start()
        drecv[g, me] = dsend[g, me]
        if g == 0:
            for each in loads[2:]:
                wait(each)
            for part in range(2):
                clear_edges(0, part)

                def relay(kk, carry):
                    i = plane(part * half + kk)
                    p = take(p_buf, i, nz)
                    press[0, i + 1] = p
                    vert[i] = take(w_buf, i, nz)
                    theta[i] = take(t_buf, i, nz)
                    keep_edges(0, part, i, p)
                    return carry

                lax.fori_loop(0, half, relay, 0, unroll=2)
                y_start(0, part)
            x_start(0)


    rows = lax.broadcasted_iota(jnp.int32, (order, order), 0)
    cols = lax.broadcasted_iota(jnp.int32, (order, order), 1)

    def source(r):
        return jnp.where(r < nz, 2 * r, 2 * (r - nz) + 1)

    pick = (cols == source(rows)).astype(F32).astype(BF16)
    wide_rows = lax.broadcasted_iota(jnp.int32, (order, classes * order), 0)
    wide_cols = lax.broadcasted_iota(jnp.int32, (order, classes * order), 1)
    for part in range(2):
        total = jnp.zeros((order, classes * order), F32)
        for c in range(classes):
            a = inv_ref[c]
            a_hi = a.astype(BF16)
            a_part = a_hi if part == 0 else (a - a_hi.astype(F32)).astype(BF16)
            by_row = jnp.dot(pick, a_part, preferred_element_type=F32).astype(BF16)
            r = wide_cols - c * order
            place = (r >= 0) & (r < order) & (wide_rows == source(r))
            total = total + jnp.dot(by_row, place.astype(F32).astype(BF16), preferred_element_type=F32)
        mats[part * order:(part + 1) * order, :] = total.astype(BF16)

    for n in range(SUBSTEPS):
        last = n == SUBSTEPS - 1
        for g in range(2):
            if not last:
                clear_edges(n + 1, g)
            if g == (0 if last else 1):
                x_wait(n)
            if last and g == 0:
                edge = press[0, nx + 1]
                for m in range(1, SUBSTEPS):
                    edge = edge + press[m, nx + 1]
                for q in range(ngy):
                    shsend[q] = edge[q * slab:(q + 1) * slab]
                for r in range(1, ngy):
                    sh_copy(r).start()
                shrecv[me] = shsend[me]
            y_wait(n, g)

            def substep(h, kk, carry):
                i = plane(h * quarter + kk)
                p = press[n, i + 1]
                up = pltpu.roll(p, ny - 1, 1)
                edge = pltpu.roll(yhalo[n, g, 0], 127 - i, 1)
                up = jnp.where(lanes == ny - 1, jnp.concatenate([edge] * (ny // 128), axis=1), up)
                down = pltpu.roll(p, 1, 1)
                edge = pltpu.roll(yhalo[n, g, 1], lax.rem(128 - i, 128), 1)
                edge = jnp.concatenate([edge] * (ny // 128), axis=1)
                edge = jnp.where(has_down, edge, p)
                down = jnp.where(lanes == 0, edge, down)
                if n == 0:
                    d = jnp.concatenate([drecv[h, q, kk] for q in range(ngy)], axis=0)
                else:
                    d = div[i]
                d = d - 0.5 * ((press[n, i + 2] - p) - (p - press[n, i]) + ((up - p) - (p - down)))
                if not last:
                    div[i] = d
                below = jnp.where(level == 0, 0.0, pltpu.roll(p, 1, 0))
                t = theta[i]
                rw = vert[i] - 0.5 * (p - below)
                rt = t - 0.5 * d
                s = jnp.concatenate([rw, rt], axis=0)
                hi = s.astype(BF16)
                lo = (s - hi.astype(F32)).astype(BF16)
                ground = terr_ref[pl.ds(i, 1), :]
                masks = [(ground == c).astype(F32).astype(BF16) for c in range(classes)]
                his = jnp.concatenate([hi * m for m in masks], axis=0)
                los = jnp.concatenate([lo * m for m in masks], axis=0)
                first = jnp.dot(mats[...], his, preferred_element_type=F32)
                second = jnp.dot(mats[:order, :], los, preferred_element_type=F32)
                solved = first[:order] + (first[order:] + second)
                st = solved[nz:]
                w = jnp.where(level >= ground, solved[:nz], 0.0)
                new_p = p - 0.3 * d + 0.5 * (st - t)
                if last:
                    put(p_buf, i, new_p)
                    put(w_buf, i, w)
                    put(t_buf, i, st)
                else:
                    press[n + 1, i + 1] = new_p
                    vert[i] = w
                    theta[i] = st
                    keep_edges(n + 1, g, i, new_p)
                if n == SUBSTEPS - 2:
                    total = new_p + p
                    for m in range(SUBSTEPS - 2):
                        total = total + press[m, i + 1]
                    for q in range(ngy):
                        ssend[h, q, kk] = total[q * slab:(q + 1) * slab]
                return carry

            for h in (2 * g, 2 * g + 1):
                if n == 0:
                    for r in range(1, ngy):
                        d_copy(h, r).wait_recv()
                lax.fori_loop(0, quarter, functools.partial(substep, h), 0, unroll=4)
                if not last and h == 2 * g + 1:
                    y_start(n + 1, g)
                    if g == 1:
                        x_start(n + 1)
                if n == SUBSTEPS - 2:
                    for r in range(1, ngy):
                        s_copy(h, r).start()
                    srecv[h, me] = ssend[h, me]

    def summed(i):
        if i == nx:
            return jnp.concatenate([shrecv[q] for q in range(ngy)], axis=1)
        g, kk = divmod((i - turn) % nx, quarter)
        return jnp.concatenate([srecv[g, q, kk] for q in range(ngy)], axis=1)

    def finish(i):
        s = summed(i)
        ahead = jnp.where(wide_lane == wide - 1, 0.0, pltpu.roll(s, wide - 1, 1))
        put(u_buf, i, take(u_buf, i, slab) - 0.5 * (summed(i + 1) - s))
        put(v_buf, i, take(v_buf, i, slab) - 0.5 * (ahead - s))

    for g in range(4):
        for r in range(1, ngy):
            s_copy(g, r).wait_recv()
        for k in range(max(g * quarter - 1, 0), (g + 1) * quarter - 1):
            if k != nx - 1 - turn:
                finish((k + turn) % nx)
    finish(turn - 1)
    for r in range(1, ngy):
        sh_copy(r).wait_recv()
    finish(nx - 1)

    pl.when(has_right)(lambda: u_copy().wait_send())
    for n in range(SUBSTEPS):
        pl.when(has_left)(lambda: x_copy(n, 0).wait_send())
        pl.when(has_right)(lambda: x_copy(n, 1).wait_send())
        for g in range(2):
            pl.when(has_down)(lambda: y_copy(n, g, 0).wait_send())
            pl.when(has_up)(lambda: y_copy(n, g, 1).wait_send())
    for r in range(1, ngy):
        for g in range(4):
            d_copy(g, r).wait_send()
            s_copy(g, r).wait_send()
        sh_copy(r).wait_send()


def write_out(*refs):
    ins, outs, sem = refs[:5], refs[5:10], refs[10]
    copies = [
        pltpu.make_async_copy(buf.at[c], out.at[:, pl.ds(c * 128, 128)], sem.at[slot, c])
        for slot, (buf, out) in enumerate(zip(ins, outs)) for c in range(buf.shape[0])]
    for each in copies:
        each.start()
    for each in copies:
        each.wait()


def per_device(wind_u, wind_v, pressure, vertical_w, theta, terrain, inverses):
    ngx, ngy = lax.axis_size("gx"), lax.axis_size("gy")
    nz, nx, ny = pressure.shape
    slab, _, wide = wind_u.shape
    classes = inverses.shape[0]
    order = 2 * nz
    quarter = nx // 4
    vmem = pl.BlockSpec(memory_space=pltpu.VMEM)
    hbm = pl.BlockSpec(memory_space=pltpu.HBM)
    slabs = jax.ShapeDtypeStruct((wide // 128, slab * nx, 128), F32)
    columns = jax.ShapeDtypeStruct((ny // 128, nz * nx, 128), F32)
    dma = pltpu.SemaphoreType.DMA
    outs = pl.pallas_call(
        functools.partial(kernel, (ngx, ngy, nz, nx, ny, slab, classes)),
        out_shape=(slabs, slabs, columns, columns, columns),
        in_specs=[hbm] * 7,
        out_specs=(vmem,) * 5,
        scratch_shapes=[
            pltpu.VMEM((nx, ny), jnp.int32),
            pltpu.VMEM((classes, order, order), F32),
            dma((5, wide // 128)), dma((2,)),
            pltpu.VMEM((SUBSTEPS, nx + 2, nz, ny), F32),
            pltpu.VMEM((nx, nz, ny), F32),
            pltpu.VMEM((nx, nz, ny), F32),
            pltpu.VMEM((nx, nz, ny), F32),
            pltpu.VMEM((4, ngy, quarter, slab, ny), F32),
            pltpu.VMEM((4, ngy, quarter, slab, ny), F32),
            pltpu.VMEM((slab, wide), F32),
            pltpu.VMEM((slab, wide), F32),
            pltpu.VMEM((SUBSTEPS, 2, 2, nz, 128), F32),
            pltpu.VMEM((SUBSTEPS, 2, 2, nz, 128), F32),
            pltpu.VMEM((4, ngy, quarter, slab, ny), F32),
            pltpu.VMEM((4, ngy, quarter, slab, ny), F32),
            pltpu.VMEM((ngy, slab, ny), F32),
            pltpu.VMEM((ngy, slab, ny), F32),
            pltpu.VMEM((2 * order, classes * order), BF16),
            dma((4, ngy)), dma((4, ngy)),
            dma((1,)), dma((1,)),
            dma((SUBSTEPS, 2, 2)), dma((SUBSTEPS, 2, 2)),
            dma((SUBSTEPS, 2)), dma((SUBSTEPS, 2)),
            dma((5, ngy)), dma((5, ngy)),
        ],
        compiler_params=pltpu.CompilerParams(
            collective_id=0, has_side_effects=True, vmem_limit_bytes=45 * 1024 * 1024),
        name="acoustic",
    )(
        wind_u.reshape(slab * nx, wide), wind_v.reshape(slab * nx, wide),
        pressure.reshape(nz * nx, ny), vertical_w.reshape(nz * nx, ny),
        theta.reshape(nz * nx, ny), terrain, inverses,
    )
    outs = pl.pallas_call(
        write_out,
        out_shape=tuple(jax.ShapeDtypeStruct((o.shape[1], o.shape[0] * 128), F32) for o in outs),
        in_specs=[vmem] * 5,
        out_specs=(hbm,) * 5,
        scratch_shapes=[dma((5, wide // 128))],
        compiler_params=pltpu.CompilerParams(vmem_limit_bytes=16 * 1024 * 1024),
        name="write_out",
    )(*outs)
    return (outs[0].reshape(slab, nx, wide), outs[1].reshape(slab, nx, wide),
            *(o.reshape(nz, nx, ny) for o in outs[2:]))


def solution(mesh):
    return jax.shard_map(
        per_device,
        mesh=mesh,
        in_specs=(
            P("gy", "gx", None),
            P("gy", "gx", None),
            P(None, "gx", "gy"),
            P(None, "gx", "gy"),
            P(None, "gx", "gy"),
            P("gx", "gy"),
            P(),
        ),
        out_specs=(
            P("gy", "gx", None),
            P("gy", "gx", None),
            P(None, "gx", "gy"),
            P(None, "gx", "gy"),
            P(None, "gx", "gy"),
        ),
        check_vma=False,
    )
```
